256 devices in a mesh: sweep: 2 (over y), row: 16 (over z), col: 4 (over x), dp: 2 (over core).
Axes of the slice: x: 4, y: 2, z: 16, core: 2. Of those that a mesh axis runs over, the one named last changes fastest.
The devices are a block of a 4x16x16 slice.
Arguments:
- token_ids: int32 [4096], P(('sweep', 'dp')), parts along dimension 0, may hold values from 0 to 15999
- sweep_index: int32 [4], P('sweep'), parts along dimension 0, may hold values from 0 to 7
- table: bfloat16 [16000, 4096], P('row', 'col'), may hold values from -6 to 6
- cotangent: bfloat16 [4096, 4096], P(('sweep', 'dp', 'row'), 'col'), parts along dimension 0, may hold values from -0.13183594 to 0.13183594
- gate_weight: bfloat16 [4096, 11008], P('col', 'row'), may hold values from -0.09375 to 0.09375
- up_weight: bfloat16 [4096, 11008], P('col', 'row'), may hold values from -0.09375 to 0.09375
- down_weight: bfloat16 [11008, 4096], P('row', 'col'), may hold values from -0.0546875 to 0.0546875
Outputs:
- grad_gate: float32 [8192, 11008], P(('sweep', 'col'), ('row', 'dp')), parts along dimension 0
- grad_up: float32 [8192, 11008], P(('sweep', 'col'), ('row', 'dp')), parts along dimension 0
- grad_down: float32 [22016, 4096], P(('sweep', 'row'), ('col', 'dp')), parts along dimension 0
The draws below stay inside these ranges and needn't reach their ends.
There are 2 independent parts, one for each index of `sweep`. The reference program is written for one: setup_inputs(seed, part) draws one part's arguments, and reference() takes and returns one part's arrays. A program takes and returns all parts, laid end to end along the dimension named above; an argument that names none is the same for every part. Nothing has to cross between parts.
All inputs are finite; a program needn't handle non-finite values.
Results may differ from the reference program's by a relative error of at most 0.0062.
Values may be sent and summed in bfloat16 or wider, within the bound.
A program may use at most 128 MiB of HBM per device.

```python
import math
import jax
import jax.numpy as jnp
import numpy as np

D = 4096
FF = 11008
VOCAB = 16000
TOKENS = 2048


def touch_ends(entries, own_key, smallest, top_value):
    dims = entries.shape
    place = [jax.random.randint(jax.random.fold_in(own_key, axis), (), 0, dims[axis]) for axis in range(len(dims))]
    entries = entries.at[tuple(place)].set(smallest)
    longest = dims.index(max(dims))
    place[longest] = (place[longest] + 1) % dims[longest]
    return entries.at[tuple(place)].set(top_value)


def levels(stream_key, extent, shards, smallest, high):
    loudness, own = 1.0, jax.random.fold_in(stream_key, 6)
    for position, blocks in shards:
        draws = jnp.exp(jax.random.uniform(jax.random.fold_in(own, position), (blocks,), jnp.float32, smallest / len(shards), high / len(shards)))
        loudness = loudness * jnp.repeat(draws, extent[position] // blocks).reshape([-1 if axis == position else 1 for axis in range(len(extent))])
    return loudness


def rank_bounds(amount, lean):
    weights = [(1 << 20) // math.isqrt(grade ** lean) + 1 for grade in range(1, amount + 1)]
    width = 1 + sum(weights) // (1 << 30)
    return np.cumsum(np.array([max(1, weight // width) for weight in weights]))


def ranked_ids(own_key, dims, amount, slope):
    listing = rank_bounds(amount, slope)
    lot = jax.random.randint(jax.random.fold_in(own_key, 1), dims, 0, int(listing[amount - 1]))
    grade = jnp.searchsorted(jnp.asarray(listing, jnp.int32), lot, side="right")
    return jax.random.permutation(jax.random.fold_in(own_key, 2), amount)[grade].astype(jnp.int32)


def noise(rng, shape, width, reach, split=(), kind=jnp.bfloat16):
    entries = width * jax.random.normal(rng, shape, jnp.float32)
    if split:
        entries = entries * levels(rng, shape, split, -0.22, 0.18)
    return jnp.clip(entries, -reach, reach).astype(kind)


def setup_inputs(seed: int = 0, part: int = 0) -> dict:
    arg_keys = jax.random.split(jax.random.key(seed), 8)
    part_keys = jax.random.split(jax.random.fold_in(arg_keys[7], part), 8)
    token_ids = touch_ends(ranked_ids(part_keys[0], (TOKENS,), VOCAB, 2), jax.random.fold_in(part_keys[0], 3), 0, VOCAB - 1).astype(jnp.int32)
    sweep_index = jax.random.randint(part_keys[1], (2,), 0, 8).astype(jnp.int32)
    table = noise(arg_keys[2], (VOCAB, D), 1.0, 6.0, ((0, 16), (1, 4)))
    cotangent = noise(part_keys[3], (TOKENS, D), (TOKENS ** -0.5), 0.13183594, ((0, 32), (1, 4)))
    gate_weight = noise(arg_keys[4], (D, FF), D ** -0.5, 0.09375, ((0, 4), (1, 16)))
    up_weight = noise(arg_keys[5], (D, FF), D ** -0.5, 0.09375, ((0, 4), (1, 16)))
    down_weight = noise(arg_keys[6], (FF, D), FF ** -0.5, 0.0546875, ((0, 16), (1, 4)))
    return {"token_ids": token_ids, "sweep_index": sweep_index, "table": table, "cotangent": cotangent, "gate_weight": gate_weight, "up_weight": up_weight, "down_weight": down_weight}


def reference(token_ids, sweep_index, table, cotangent, gate_weight, up_weight, down_weight):
    k_input = sweep_index[0].astype(jnp.float32)
    k_output = sweep_index[1].astype(jnp.float32)
    in_mult = jnp.exp2(k_input / 2.0 - 1.5)
    out_mult = jnp.exp2(1.0 - k_output / 2.0)
    embedded = jnp.take(table, token_ids, axis=0)
    scaled = (in_mult * embedded.astype(jnp.float32)).astype(jnp.bfloat16)
    gate = jnp.dot(scaled, gate_weight, preferred_element_type=jnp.float32)
    up = jnp.dot(scaled, up_weight, preferred_element_type=jnp.float32)
    back = out_mult * jnp.dot(cotangent, down_weight.T, preferred_element_type=jnp.float32)
    sig = jax.nn.sigmoid(gate)
    silu = gate * sig
    hidden = (silu * up).astype(jnp.bfloat16)
    d_gate = (back * up * sig * (1.0 + gate * (1.0 - sig))).astype(jnp.bfloat16)
    d_up = (back * silu).astype(jnp.bfloat16)
    grad_down = out_mult * jnp.dot(hidden.T, cotangent, preferred_element_type=jnp.float32)
    grad_gate = jnp.dot(scaled.T, d_gate, preferred_element_type=jnp.float32)
    grad_up = jnp.dot(scaled.T, d_up, preferred_element_type=jnp.float32)
    return grad_gate, grad_up, grad_down
```

```python
import functools

import jax
import jax.numpy as jnp
from jax import lax
from jax.experimental import pallas as pl
from jax.experimental.pallas import tpu as pltpu
from jax.sharding import PartitionSpec as P

MESH = pl.DeviceIdType.MESH
BF16 = jnp.bfloat16
F32 = jnp.float32
LANES = 128
PACK = 16


def up_to(n, m):
    return -(-n // m) * m


def dot_nt(a, b):
    return lax.dot_general(a, b, (((1,), (1,)), ((), ())), preferred_element_type=F32)


def dot_nn(a, b):
    return lax.dot_general(a, b, (((1,), (0,)), ((), ())), preferred_element_type=F32)


def arrival_order(nz):
    order = [0]
    for s in range(1, nz // 2):
        order += [-s, s]
    return order + [nz // 2]


def kernel(
    nz, nx, hid,
    ids_ref, mult_ref, table_ref, cot_ref, w_ref,
    gg_ref, gu_ref, gd_ref,
    look, rs_left, rs_right, xs, cs, xt, p32, p16, relay, comb, arrived, acts, gd_acc, gd_other,
    rs_send, rs_recv, ag_send, ag_recv, dp_send, dp_recv, xr_send, xr_recv, xg_send, xg_recv, gd_sem,
):
    z, x, c = lax.axis_index("row"), lax.axis_index("col"), lax.axis_index("dp")
    up_z, down_z = lax.rem(z + 1, nz), lax.rem(z + nz - 1, nz)
    right, left, far = lax.rem(x + 1, nx), lax.rem(x + nx - 1, nx), lax.rem(x + 2, nx)
    other = 1 - c
    half = nz // 2
    order = arrival_order(nz)
    slot_of = {d % nz: p for p, d in enumerate(order)}
    groups = nz // nx
    width = p32.shape[2] // 3
    mid = p32.shape[2] // 2
    rows = cot_ref.shape[0]
    part = rows // 2
    in_mult, out_mult = mult_ref[0], mult_ref[1]
    pending = []

    def send(src, dst, ssem, rsem, **where):
        copy = pltpu.make_async_remote_copy(
            src_ref=src, dst_ref=dst, send_sem=ssem, recv_sem=rsem,
            device_id=where, device_id_type=MESH,
        )
        copy.start()
        pending.append(copy)

    def landed(dst, rsem):
        pltpu.make_async_remote_copy(
            src_ref=dst, dst_ref=dst, send_sem=rsem, recv_sem=rsem,
            device_id={"dp": other}, device_id_type=MESH,
        ).wait_recv()

    def lookup(offsets):
        picks = []
        for d in offsets:
            ids = ids_ref[lax.rem(z + d + nz, nz)]
            spot = lax.broadcasted_iota(jnp.int32, (rows, table_ref.shape[0]), 1)
            picks.append(jnp.where(spot == ids[:, 0:1], 1.0, 0.0).astype(BF16))
        hot = picks[0] if len(picks) == 1 else jnp.concatenate(picks, axis=0)
        found = dot_nn(hot, table_ref[...])
        scaled = (in_mult * found).astype(BF16)
        for n, d in enumerate(offsets):
            look[d % nz] = scaled[n * rows : (n + 1) * rows]

    barrier = pltpu.get_barrier_semaphore()
    for where in ({"row": up_z}, {"row": down_z}, {"col": left}, {"col": right}, {"dp": other}):
        pl.semaphore_signal(barrier, inc=1, device_id=where, device_id_type=MESH)
    lookup((-half, half - 1))
    pl.semaphore_wait(barrier, 5)

    for s in range(1, half + 1):
        down_d, up_d = s - 1 - half, half - s
        if s > 1:
            lookup((down_d, up_d) if s < half else (down_d, 0))
        for h in range(2):
            cut = pl.ds(h * part, part)
            if s > 1:
                landed(rs_left.at[s - 2, cut], rs_recv.at[0, s - 2, h])
                look[down_d % nz, cut] = look[down_d % nz, cut] + rs_left[s - 2, cut]
            send(look.at[down_d % nz, cut], rs_left.at[s - 1, cut],
                 rs_send.at[0, s - 1, h], rs_recv.at[0, s - 1, h], row=down_z)
            if s < half:
                if s > 1:
                    landed(rs_right.at[s - 2, cut], rs_recv.at[1, s - 2, h])
                    look[up_d % nz, cut] = look[up_d % nz, cut] + rs_right[s - 2, cut]
                send(look.at[up_d % nz, cut], rs_right.at[s - 1, cut],
                     rs_send.at[1, s - 1, h], rs_recv.at[1, s - 1, h], row=up_z)

    for h in range(2):
        cut = pl.ds(h * part, part)
        landed(rs_left.at[half - 1, cut], rs_recv.at[0, half - 1, h])
        landed(rs_right.at[half - 2, cut], rs_recv.at[1, half - 2, h])
        xs[0, c, cut] = look[0, cut] + rs_left[half - 1, cut] + rs_right[half - 2, cut]
    cs[0, c] = cot_ref[...]

    bufs = (cs, xs)

    def spread(k, slot, step, go_up, go_down):
        buf = bufs[k]
        send(buf.at[slot, c], buf.at[slot, c], dp_send.at[k, slot], dp_recv.at[k, slot], dp=other)
        for way, go, where in ((0, go_up, up_z), (1, go_down, down_z)):
            if go:
                d = -(step + 1) if way == 0 else step + 1
                to = slot_of[d % nz]
                send(buf.at[slot, c], buf.at[to, c], ag_send.at[k, way, step], ag_recv.at[k, way, step], row=where)

    reach = ((half, half - 1), (half - 1, half))

    def ring_step(k, s):
        up_n, down_n = reach[k]
        if s <= up_n:
            slot = slot_of[(-s) % nz]
            landed(bufs[k].at[slot, c], ag_recv.at[k, 0, s - 1])
            spread(k, slot, s, s < up_n, False)
        if s <= down_n:
            slot = slot_of[s % nz]
            landed(bufs[k].at[slot, c], ag_recv.at[k, 1, s - 1])
            spread(k, slot, s, False, s < down_n)

    def forward(g):
        for i in range(nx):
            for k in range(2):
                slot = g * nx + i
                landed(bufs[k].at[slot, other], dp_recv.at[k, slot])
        step = width // 2

        def rows_of(buf, first, t, carry):
            at = pl.ds(pl.multiple_of(first + t * step, PACK), step)
            tokens = buf[g * nx : (g + 1) * nx].reshape(nx * 2 * rows, buf.shape[-1])
            val = dot_nt(w_ref[at], tokens)
            for i in range(nx):
                block = val[:, i * 2 * rows : (i + 1) * 2 * rows]
                p32[g, i, at] = block
                p16[g, i, at] = block.astype(BF16)
            return carry

        lax.fori_loop(0, 4, functools.partial(rows_of, xs, 0), 0)
        lax.fori_loop(0, 2, functools.partial(rows_of, cs, 2 * width), 0)

    top, low = pl.ds(0, mid), pl.ds(mid, mid)

    def sums_start(g):
        send(p16.at[g, far, top], relay.at[g, 0], xr_send.at[g, 0], xr_recv.at[g, 0], col=right)
        send(p16.at[g, far, low], relay.at[g, 1], xr_send.at[g, 1], xr_recv.at[g, 1], col=left)
        send(p16.at[g, right, low], arrived.at[g, 0, low], xr_send.at[g, 2], xr_recv.at[g, 2], col=right)
        send(p16.at[g, left, top], arrived.at[g, 1, top], xr_send.at[g, 3], xr_recv.at[g, 3], col=left)

    def sums_relay(g):
        landed(relay.at[g, 0], xr_recv.at[g, 0])
        comb[g, 0] = (p32[g, right, top] + relay[g, 0].astype(F32)).astype(BF16)
        send(comb.at[g, 0], arrived.at[g, 0, top], xr_send.at[g, 4], xr_recv.at[g, 4], col=right)
        landed(relay.at[g, 1], xr_recv.at[g, 1])
        comb[g, 1] = (p32[g, left, low] + relay[g, 1].astype(F32)).astype(BF16)
        send(comb.at[g, 1], arrived.at[g, 1, low], xr_send.at[g, 5], xr_recv.at[g, 5], col=left)

    def activate(g):
        landed(arrived.at[g, 0, low], xr_recv.at[g, 2])
        landed(arrived.at[g, 1, top], xr_recv.at[g, 3])
        landed(arrived.at[g, 0, top], xr_recv.at[g, 4])
        landed(arrived.at[g, 1, low], xr_recv.at[g, 5])

        def total(n):
            at = pl.ds(n * width, width)
            return p32[g, x, at] + arrived[g, 0, at].astype(F32) + arrived[g, 1, at].astype(F32)

        gate, up, back = total(0), total(1), out_mult * total(2)
        sig = jax.nn.sigmoid(gate)
        silu = gate * sig
        acts[g, x, 0:width] = (silu * up).astype(BF16)
        acts[g, x, width : 2 * width] = (back * up * sig * (1.0 + gate * (1.0 - sig))).astype(BF16)
        acts[g, x, 2 * width : 3 * width] = (back * silu).astype(BF16)
        send(acts.at[g, x], acts.at[g, x], xg_send.at[g, 0], xg_recv.at[g, 0], col=right)
        send(acts.at[g, x], acts.at[g, x], xg_send.at[g, 1], xg_recv.at[g, 1], col=left)

    def acts_relay(g):
        landed(acts.at[g, left], xg_recv.at[g, 0])
        send(acts.at[g, left, top], acts.at[g, left, top], xg_send.at[g, 2], xg_recv.at[g, 2], col=right)
        landed(acts.at[g, right], xg_recv.at[g, 1])
        send(acts.at[g, right, low], acts.at[g, right, low], xg_send.at[g, 3], xg_recv.at[g, 3], col=left)

    def transposed(g):
        for i in range(nx):
            block = xs[g * nx + i].reshape(2 * rows, xs.shape[-1])
            xt[g, :, i * 2 * rows : (i + 1) * 2 * rows] = block.T

    def joined(g, n):
        at = pl.ds(n * width, width)
        return jnp.concatenate([acts[g, q, at] for q in range(nx)], axis=1)

    def gradients(g):
        landed(acts.at[g, far, top], xg_recv.at[g, 2])
        landed(acts.at[g, far, low], xg_recv.at[g, 3])
        quarter = gd_acc.shape[2] // 2

        def down(t, carry):
            h, n = t // 2, lax.rem(t, 2)
            feats = pl.ds(pl.multiple_of(t * quarter, LANES), quarter)
            tokens = cs[g * nx : (g + 1) * nx, :, :, feats].reshape(nx * 2 * rows, quarter)
            val = dot_nn(joined(g, 0), tokens)[:hid]
            to = pl.ds(pl.multiple_of(n * quarter, LANES), quarter)
            if g > 0:
                val = val + gd_acc[h, :, to]
            gd_acc[h, :, to] = out_mult * val if g == groups - 1 else val
            return carry

        lax.fori_loop(0, 4, down, 0)
        if g == groups - 1:
            send(gd_acc.at[other], gd_other, gd_sem.at[0], gd_sem.at[1], dp=other)

        tile = gg_ref.shape[0] // 4
        for n, out in ((1, gg_ref), (2, gu_ref)):

            def side(n, out, t, carry):
                at = pl.ds(pl.multiple_of(t * tile, tile), tile)
                val = dot_nt(xt[g, at], joined(g, n))[:, :hid]
                out[at] = val if g == 0 else out[at] + val
                return carry

            lax.fori_loop(0, 4, functools.partial(side, n, out), 0)

    spread(0, 0, 0, True, True)
    spread(1, 0, 0, True, True)
    later = {}

    def plan(tick, *calls):
        later.setdefault(tick, []).extend(calls)

    for g in range(groups):
        t = 2 * g + 2
        plan(t, (forward, g), (sums_start, g), (transposed, g))
        plan(t + 1, (sums_relay, g))
        plan(t + 2, (activate, g))
        plan(t + 3, (acts_relay, g))
        plan(t + 4, (gradients, g))
    for tick in range(1, max(later) + 1):
        if tick <= half:
            ring_step(0, tick)
            ring_step(1, tick)
        for call, g in reversed(later.get(tick, [])) if False else later.get(tick, []):
            call(g)

    landed(gd_other, gd_sem.at[1])
    gd_ref[pl.ds(pl.multiple_of(c * hid, 8), hid)] = gd_acc[c]
    gd_ref[pl.ds(pl.multiple_of(other * hid, 8), hid)] = gd_other[...]
    for copy in pending:
        copy.wait_send()


def solution(mesh):
    nz, nx, nc = mesh.shape["row"], mesh.shape["col"], mesh.shape["dp"]

    def local(token_ids, sweep_index, table, cotangent, gate_weight, up_weight, down_weight):
        hid = gate_weight.shape[1] // nc
        feat = table.shape[1]
        rows = cotangent.shape[0]
        width = up_to(hid, 2 * PACK)
        k = sweep_index.astype(F32)
        mult = jnp.stack([jnp.exp2(k[0] / 2.0 - 1.5), jnp.exp2(1.0 - k[1] / 2.0)])
        ids = token_ids - lax.axis_index("row") * table.shape[0]
        ids = jnp.broadcast_to(ids.reshape(nz, rows, 1), (nz, rows, LANES))
        at = lax.axis_index("dp") * hid

        def padded(w):
            return jnp.pad(w, ((0, width - hid), (0, 0)))

        weights = jnp.concatenate([
            padded(lax.dynamic_slice_in_dim(gate_weight, at, hid, 1).T),
            padded(lax.dynamic_slice_in_dim(up_weight, at, hid, 1).T),
            padded(lax.dynamic_slice_in_dim(down_weight, at, hid, 0)),
        ], axis=0)
        groups, half, slots = nz // nx, nz // 2, nz
        tall, lanes = 3 * width, nc * rows
        dma = pltpu.SemaphoreType.DMA
        vmem = pl.BlockSpec(memory_space=pltpu.VMEM)
        return pl.pallas_call(
            functools.partial(kernel, nz, nx, hid),
            out_shape=(
                jax.ShapeDtypeStruct((feat, hid), F32),
                jax.ShapeDtypeStruct((feat, hid), F32),
                jax.ShapeDtypeStruct((nc * hid, feat // nc), F32),
            ),
            in_specs=[vmem, pl.BlockSpec(memory_space=pltpu.SMEM), vmem, vmem, vmem],
            out_specs=(vmem, vmem, vmem),
            scratch_shapes=[
                pltpu.VMEM((nz, rows, feat), BF16),
                pltpu.VMEM((half, rows, feat), BF16),
                pltpu.VMEM((half, rows, feat), BF16),
                pltpu.VMEM((slots, nc, rows, feat), BF16),
                pltpu.VMEM((slots, nc, rows, feat), BF16),
                pltpu.VMEM((groups, feat, nx * lanes), BF16),
                pltpu.VMEM((groups, nx, tall, lanes), F32),
                pltpu.VMEM((groups, nx, tall, lanes), BF16),
                pltpu.VMEM((groups, 2, tall // 2, lanes), BF16),
                pltpu.VMEM((groups, 2, tall // 2, lanes), BF16),
                pltpu.VMEM((groups, 2, tall, lanes), BF16),
                pltpu.VMEM((groups, nx, tall, lanes), BF16),
                pltpu.VMEM((nc, hid, feat // nc), F32),
                pltpu.VMEM((hid, feat // nc), F32),
                dma((2, half, 2)), dma((2, half, 2)),
                dma((2, 2, half)), dma((2, 2, half)),
                dma((2, slots)), dma((2, slots)),
                dma((groups, 6)), dma((groups, 6)),
                dma((groups, 4)), dma((groups, 4)),
                dma((2,)),
            ],
            compiler_params=pltpu.CompilerParams(
                collective_id=0, has_side_effects=True, vmem_limit_bytes=64 * 1024 * 1024 - 65536,
            ),
        )(ids, mult, table, cotangent, weights)

    return jax.shard_map(
        local,
        mesh=mesh,
        in_specs=(
            P(("sweep", "dp")),
            P("sweep"),
            P("row", "col"),
            P(("sweep", "dp", "row"), "col"),
            P("col", "row"),
            P("col", "row"),
            P("row", "col"),
        ),
        out_specs=(
            P(("sweep", "col"), ("row", "dp")),
            P(("sweep", "col"), ("row", "dp")),
            P(("sweep", "row"), ("col", "dp")),
        ),
        check_vma=False,
    )
```

```python
import functools

import jax
import jax.numpy as jnp
from jax import lax
from jax.experimental import pallas as pl
from jax.experimental.pallas import tpu as pltpu
from jax.sharding import PartitionSpec as P

MESH = pl.DeviceIdType.MESH
BF16 = jnp.bfloat16
F32 = jnp.float32
LANES = 128
PACK = 16


FIRST = (
    "",
    "",
    "| w1",
    "| w2",
    "| w0",
    "",
    "",
    "",
)
SECOND = (
    "x0",
    "x1",
    "x2 fS0 c0",
    "x3 c1 fR0",
    "c2 fF0 bS0",
    "x4 c3 bR0 fS1 fP0 bF0",
    "x5 c4 fR1 bP0",
    "c5 bS1 fF1 x6 c6 bR1 fS2 fP1 bF1",
    "x7 c7 fR2 bS2 bP1 fF2",
    "x8 c8 bR2 bS3 fS3 fP2 bF2 G0",
    "bR3 fR3 G1 bP2 bF3 fF3 G2",
    "bP3 fP3 A3 G3",
)


TURN = (0, 1, 2, 2, 2, 2, 3, 4, 5, 5)


def up_to(n, m):
    return -(-n // m) * m


def dot_nt(a, b):
    return lax.dot_general(a, b, (((1,), (1,)), ((), ())), preferred_element_type=F32)


def dot_nn(a, b):
    return lax.dot_general(a, b, (((1,), (0,)), ((), ())), preferred_element_type=F32)


def arrival_order(nz):
    order = [0]
    for s in range(1, nz // 2):
        order += [-s, s]
    return order + [nz // 2]


def kernel(
    nz, nx, hid,
    ids_ref, index_ref, table_hbm, cot_ref, gate_hbm, up_hbm, down_hbm,
    gg_ref, gu_ref, gd_ref,
    ids, table_ref, gate_w, up_w, down_w, w, look, rs_left, rs_right, xs, cs,
    bp32, bp16, brelay, bcomb, barrived, bsum,
    fp32, fp16, frelay, fcomb, farrived, fsum,
    acts, hid_other,
    t_sem, w_sem, rs_send, rs_recv, c_send, c_recv, x_send, x_recv, dp_send, dp_recv,
    br_send, br_recv, fr_send, fr_recv, hid_send, hid_recv,
):
    z, x, c = lax.axis_index("row"), lax.axis_index("col"), lax.axis_index("dp")
    up_z, down_z = lax.rem(z + 1, nz), lax.rem(z + nz - 1, nz)
    right, left, far = lax.rem(x + 1, nx), lax.rem(x + nx - 1, nx), lax.rem(x + 2, nx)
    other = 1 - c
    half = nz // 2
    order = arrival_order(nz)
    slot_of = {d % nz: p for p, d in enumerate(order)}
    groups = nz // nx
    width = bp32.shape[2]
    rows = cot_ref.shape[0]
    feat = cot_ref.shape[1]
    lanes = 2 * rows
    fetches = [
        pltpu.make_async_copy(src, dst, w_sem.at[n])
        for n, (src, dst) in enumerate(((down_hbm, down_w), (gate_hbm, gate_w), (up_hbm, up_w)))
    ]
    entries = table_hbm.shape[0]
    step = up_to(entries // 8, 8)
    parts = [
        pltpu.make_async_copy(table_hbm.at[a : min(a + step, entries)], table_ref.at[a : min(a + step, entries)], t_sem.at[n])
        for n, a in enumerate(range(0, entries, step))
    ]
    for copy in parts:
        copy.start()

    def send(src, dst, ssem, rsem, **where):
        copy = pltpu.make_async_remote_copy(
            src_ref=src, dst_ref=dst, send_sem=ssem, recv_sem=rsem,
            device_id=where, device_id_type=MESH,
        )
        copy.start()

    def sent(ref, ssem):
        pltpu.make_async_remote_copy(
            src_ref=ref, dst_ref=ref, send_sem=ssem, recv_sem=ssem,
            device_id={"dp": other}, device_id_type=MESH,
        ).wait_send()

    def landed(dst, rsem):
        pltpu.make_async_remote_copy(
            src_ref=dst, dst_ref=dst, send_sem=rsem, recv_sem=rsem,
            device_id={"dp": other}, device_id_type=MESH,
        ).wait_recv()

    barrier = pltpu.get_barrier_semaphore()
    for where in ({"row": up_z}, {"row": down_z}, {"col": left}, {"col": right}, {"dp": other}):
        pl.semaphore_signal(barrier, inc=1, device_id=where, device_id_type=MESH)

    for t in range(ids_ref.shape[0]):
        wide = jnp.broadcast_to(ids_ref[t : t + 1], (LANES, LANES))
        ids[t * LANES : (t + 1) * LANES] = wide.T - z * table_ref.shape[0]
    k_in = jnp.full((1, feat), index_ref[0].astype(F32), F32)
    k_out = jnp.full((1, LANES), index_ref[1].astype(F32), F32)
    in_mult = jnp.exp2(k_in / 2.0 - 1.5)
    out_mult = jnp.exp2(1.0 - k_out / 2.0)

    def lookup(offsets):
        picks = []
        for d in offsets:
            at = pl.ds(pl.multiple_of(lax.rem(z + d + nz, nz) * rows, rows), rows)
            wide = jnp.concatenate([ids[at]] * (up_to(entries, LANES) // LANES), axis=1)[:, :entries]
            spot = lax.broadcasted_iota(jnp.int32, (rows, entries), 1)
            picks.append(jnp.where(spot == wide, 1.0, 0.0).astype(BF16))
        found = dot_nn(jnp.concatenate(picks, axis=0), table_ref[...])
        scaled = (in_mult * found).astype(BF16)
        for n, d in enumerate(offsets):
            look[d % nz] = scaled[n * rows : (n + 1) * rows]

    for copy in parts:
        copy.wait()
    for fetch in fetches:
        fetch.start()
    lookup((-half, half - 1))
    cs[0, c] = cot_ref[...]
    pl.semaphore_wait(barrier, 5)

    c_up, c_down = half, half - 1
    x_up, x_down = half - 1, half
    ways = ((0, up_z), (1, down_z))

    def slot_at(way, s):
        return slot_of[(-s if way == 0 else s) % nz]

    def c_ring(s):
        for way, where in ways:
            n = (c_up, c_down)[way]
            if s > n:
                continue
            slot = slot_at(way, s)
            if s > 0:
                landed(cs.at[slot, c], c_recv.at[way, s - 1])
            if s > 0 or way == 0:
                send(cs.at[slot, c], cs.at[slot, c], dp_send.at[0], dp_recv.at[0, slot // nx], dp=other)
            if s < n:
                send(cs.at[slot, c], cs.at[slot_at(way, s + 1), c], c_send.at[0], c_recv.at[way, s], row=where)

    def x_ring(s):
        for h in range(2):
            cut = pl.ds(h * (rows // 2), rows // 2)
            for way, where in ways:
                n = (x_up, x_down)[way]
                if s > n:
                    continue
                slot = slot_at(way, s)
                if s > 0:
                    landed(xs.at[slot, c, cut], x_recv.at[way, s - 1, h])
                if s > 0 or way == 0:
                    send(xs.at[slot, c, cut], xs.at[slot, c, cut], dp_send.at[1], dp_recv.at[1, slot // nx], dp=other)
                if s < n:
                    send(xs.at[slot, c, cut], xs.at[slot_at(way, s + 1), c, cut],
                         x_send.at[0], x_recv.at[way, s, h], row=where)

    class Sums:
        def __init__(self, kind, first, bufs, sems, tokens):
            self.kind, self.first, self.tokens = kind, first, tokens
            self.p32, self.p16, self.relay, self.comb, self.arrived, self.sum = bufs
            self.ssem, self.rsem = sems
            self.tall = self.p32.shape[2]
            self.top, self.low = pl.ds(0, self.tall // 2), pl.ds(self.tall // 2, self.tall // 2)

        def go(self, g, n, src, dst, **where):
            send(src, dst, self.ssem.at[1 if n in (6, 7) else 0], self.rsem.at[g, TURN[n]], **where)

        def got(self, g, n, dst):
            landed(dst, self.rsem.at[g, TURN[n]])

        def start(self, g):
            landed(self.tokens.at[g * nx : (g + 1) * nx, other], dp_recv.at[self.kind, g])
            pair = 2

            def tokens_of(t, carry):
                tokens = self.tokens[pl.ds(g * nx + t * pair, pair)].reshape(pair * lanes, feat)
                val = dot_nt(w[self.first : self.first + self.tall], tokens)
                for i in range(pair):
                    block = val[:, i * lanes : (i + 1) * lanes]
                    self.p32[g, t * pair + i] = block
                    self.p16[g, t * pair + i] = block.astype(BF16)
                return carry

            lax.fori_loop(0, nx // pair, tokens_of, 0)
            top, low = self.top, self.low
            self.go(g, 0, self.p16.at[g, far, top], self.relay.at[g, 0], col=right)
            self.go(g, 1, self.p16.at[g, far, low], self.relay.at[g, 1], col=left)
            self.go(g, 2, self.p16.at[g, right, low], self.arrived.at[g, 0, low], col=right)
            self.go(g, 3, self.p16.at[g, left, top], self.arrived.at[g, 1, top], col=left)

        def relay_sums(self, g):
            top, low = self.top, self.low
            self.got(g, 0, self.relay.at[g, 0])
            self.comb[g, 0] = (self.p32[g, right, top] + self.relay[g, 0].astype(F32)).astype(BF16)
            self.go(g, 4, self.comb.at[g, 0], self.arrived.at[g, 0, top], col=right)
            self.got(g, 1, self.relay.at[g, 1])
            self.comb[g, 1] = (self.p32[g, left, low] + self.relay[g, 1].astype(F32)).astype(BF16)
            self.go(g, 5, self.comb.at[g, 1], self.arrived.at[g, 1, low], col=left)

        def finish(self, g):
            self.got(g, 2, self.arrived.at[g])
            total = self.p32[g, x] + self.arrived[g, 0].astype(F32) + self.arrived[g, 1].astype(F32)
            if self.kind == 0:
                total = out_mult[:, :lanes] * total
            self.sum[g, x] = total.astype(BF16)
            self.go(g, 6, self.sum.at[g, x], self.sum.at[g, x], col=right)
            self.go(g, 7, self.sum.at[g, x], self.sum.at[g, x], col=left)

        def pass_on(self, g):
            top, low = self.top, self.low
            self.got(g, 6, self.sum.at[g, left])
            self.go(g, 8, self.sum.at[g, left, top], self.sum.at[g, left, top], col=right)
            self.got(g, 7, self.sum.at[g, right])
            self.go(g, 9, self.sum.at[g, right, low], self.sum.at[g, right, low], col=left)

        def gathered(self, g):
            self.got(g, 8, self.sum.at[g, far])

        def drained(self):
            sent(self.p16, self.ssem.at[0])
            sent(self.arrived, self.ssem.at[1])

    back_sums = Sums(0, 2 * width, (bp32, bp16, brelay, bcomb, barrived, bsum), (br_send, br_recv), cs)
    fwd_sums = Sums(1, 0, (fp32, fp16, frelay, fcomb, farrived, fsum), (fr_send, fr_recv), xs)

    def weight_rows(n, src, first):
        fetches[n].wait()
        w[first + width - PACK : first + width] = jnp.zeros((PACK, feat), BF16)
        for core in range(2):

            @pl.when(c == core)
            def _():
                mine = slice(core * hid, (core + 1) * hid)
                w[first : first + hid] = src[mine]

    def activate(g, q):
        gate = fsum[g, q, :width].astype(F32)
        up = fsum[g, q, width:].astype(F32)
        back = bsum[g, q].astype(F32)
        sig = jax.nn.sigmoid(gate)
        silu = gate * sig
        acts[g, q, :width] = (silu * up).astype(BF16)
        acts[g, q, width : 2 * width] = (back * up * sig * (1.0 + gate * (1.0 - sig))).astype(BF16)
        acts[g, q, 2 * width :] = (back * silu).astype(BF16)
        send(acts.at[g, q, 0:width], hid_other.at[g, q], hid_send.at[0], hid_recv.at[g], dp=other)

    def near_activations(g):
        back_sums.gathered(g)

        def one(t, carry):
            activate(g, lax.rem(x + nx - 1 + t, nx))
            return carry

        lax.fori_loop(0, nx - 1, one, 0)

    def gradients(g):
        last = g == groups - 1
        if not last:
            near_activations(g)
        fwd_sums.gathered(g)
        activate(g, far)
        quarter = feat // 4
        slots = slice(g * nx, (g + 1) * nx)

        def product(left_side, tokens, feats):
            return dot_nn(left_side, tokens[slots, :, :, feats].reshape(nx * lanes, quarter))

        def along_tokens(pieces):
            return jnp.concatenate(pieces, axis=1)

        def sides(t, carry):
            feats = pl.ds(pl.multiple_of(t * quarter, LANES), quarter)
            val = product(along_tokens([acts[g, q, width:] for q in range(nx)]), xs, feats)
            for out, first in ((gg_ref, 0), (gu_ref, width)):
                part = val[first : first + hid]
                out[:, feats] = part if g == 0 else out[:, feats] + part
            return carry

        lax.fori_loop(0, 4, sides, 0)
        landed(hid_other.at[g], hid_recv.at[g])

        def down(t, carry):
            feats = pl.ds(pl.multiple_of((2 * c + t) * quarter, LANES), quarter)
            to = pl.ds(pl.multiple_of(t * quarter, LANES), quarter)
            mine = along_tokens([acts[g, q, :width] for q in range(nx)])
            theirs = along_tokens([hid_other[g, q] for q in range(nx)])
            val = product(jnp.concatenate([mine, theirs], axis=0), cs, feats)
            for core, first in ((c, 0), (other, width)):
                at = pl.ds(pl.multiple_of(core * hid, 8), hid)
                part = val[first : first + hid]
                if g > 0:
                    part = part + gd_ref[at, to]
                gd_ref[at, to] = out_mult[:, :1] * part if last else part
            return carry

        lax.fori_loop(0, 2, down, 0)

    pieces = 4
    part = rows // pieces

    def rs_step(s):
        down_d, up_d = s - 1 - half, half - s
        for h in range(pieces):
            cut = pl.ds(h * part, part)
            if s > 1:
                landed(rs_left.at[s - 2, cut], rs_recv.at[0, s - 2, h])
                look[down_d % nz, cut] = look[down_d % nz, cut] + rs_left[s - 2, cut]
            send(look.at[down_d % nz, cut], rs_left.at[s - 1, cut],
                 rs_send.at[0], rs_recv.at[0, s - 1, h], row=down_z)
            if s < half:
                if s > 1:
                    landed(rs_right.at[s - 2, cut], rs_recv.at[1, s - 2, h])
                    look[up_d % nz, cut] = look[up_d % nz, cut] + rs_right[s - 2, cut]
                send(look.at[up_d % nz, cut], rs_right.at[s - 1, cut],
                     rs_send.at[1], rs_recv.at[1, s - 1, h], row=up_z)

    calls = {
        "w": lambda g: weight_rows(*((0, down_w, 2 * width), (1, gate_w, 0), (2, up_w, width))[g]),
        "c": c_ring, "x": x_ring, "A": near_activations, "G": gradients,
        "bS": back_sums.start, "bR": back_sums.relay_sums, "bF": back_sums.finish, "bP": back_sums.pass_on,
        "fS": fwd_sums.start, "fR": fwd_sums.relay_sums, "fF": fwd_sums.finish, "fP": fwd_sums.pass_on,
    }

    def run(line):
        for item in line.split():
            name, n = item[:-1], int(item[-1])
            calls[name](n)

    for s in range(1, half + 1):
        rs_step(s)
        run(FIRST[s - 1].partition("|")[0])
        if s < half:
            lookup((s - half, half - s - 1))
        run(FIRST[s - 1].partition("|")[2])

    for h in range(pieces):
        cut = pl.ds(h * part, part)
        landed(rs_left.at[half - 1, cut], rs_recv.at[0, half - 1, h])
        landed(rs_right.at[half - 2, cut], rs_recv.at[1, half - 2, h])
        xs[0, c, cut] = look[0, cut] + rs_left[half - 1, cut] + rs_right[half - 2, cut]
    for line in SECOND:
        run(line)

    sent(rs_left, rs_send.at[0])
    sent(rs_right.at[: half - 1], rs_send.at[1])
    for sem in (c_send, x_send):
        sent(look.at[: nz - 1], sem.at[0])
    for k in range(2):
        sent(look, dp_send.at[k])
    back_sums.drained()
    fwd_sums.drained()
    sent(hid_other, hid_send.at[0])


def solution(mesh):
    nz, nx, nc = mesh.shape["row"], mesh.shape["col"], mesh.shape["dp"]

    def local(token_ids, sweep_index, table, cotangent, gate_weight, up_weight, down_weight):
        hid = gate_weight.shape[1] // nc
        feat = table.shape[1]
        rows = cotangent.shape[0]
        width = up_to(hid, 2 * PACK)
        groups, half, slots = nz // nx, nz // 2, nz
        lanes = nc * rows
        dma = pltpu.SemaphoreType.DMA
        vmem = pl.BlockSpec(memory_space=pltpu.VMEM)
        smem = pl.BlockSpec(memory_space=pltpu.SMEM)
        hbm = pl.BlockSpec(memory_space=pl.ANY)

        def sums(tall):
            return [
                pltpu.VMEM((groups, nx, tall, lanes), F32),
                pltpu.VMEM((groups, nx, tall, lanes), BF16),
                pltpu.VMEM((groups, 2, tall // 2, lanes), BF16),
                pltpu.VMEM((groups, 2, tall // 2, lanes), BF16),
                pltpu.VMEM((groups, 2, tall, lanes), BF16),
                pltpu.VMEM((groups, nx, tall, lanes), BF16),
            ]

        shapes = ((hid, feat), (hid, feat), (nc * hid, feat // nc))
        grad_gate, grad_up, grad_down = pl.pallas_call(
            functools.partial(kernel, nz, nx, hid),
            out_shape=tuple(pltpu.VMEM(shape, F32) for shape in shapes),
            in_specs=[vmem, smem, hbm, vmem, hbm, hbm, hbm],
            out_specs=(vmem, vmem, vmem),
            scratch_shapes=[
                pltpu.VMEM((nz * rows, LANES), jnp.int32),
                pltpu.VMEM(table.shape, BF16),
                pltpu.VMEM(down_weight.shape, BF16),
                pltpu.VMEM(down_weight.shape, BF16),
                pltpu.VMEM(down_weight.shape, BF16),
                pltpu.VMEM((3 * width, feat), BF16),
                pltpu.VMEM((nz, rows, feat), BF16),
                pltpu.VMEM((half, rows, feat), BF16),
                pltpu.VMEM((half, rows, feat), BF16),
                pltpu.VMEM((slots, nc, rows, feat), BF16),
                pltpu.VMEM((slots, nc, rows, feat), BF16),
                *sums(width),
                *sums(2 * width),
                pltpu.VMEM((groups, nx, 3 * width, lanes), BF16),
                pltpu.VMEM((groups, nx, width, lanes), BF16),
                dma((8,)), dma((3,)),
                dma((2,)), dma((2, half, 4)),
                dma((1,)), dma((2, half)),
                dma((1,)), dma((2, half, 2)),
                dma((2,)), dma((2, groups)),
                dma((2,)), dma((groups, 6)),
                dma((2,)), dma((groups, 6)),
                dma((1,)), dma((groups,)),
            ],
            compiler_params=pltpu.CompilerParams(
                collective_id=0, has_side_effects=True, vmem_limit_bytes=58 * 1024 * 1024,
            ),
        )(token_ids.reshape(-1, LANES), sweep_index, table, cotangent, gate_weight.T, up_weight.T, down_weight)
        return grad_gate.T, grad_up.T, grad_down

    return jax.shard_map(
        local,
        mesh=mesh,
        in_specs=(
            P(("sweep", "dp")),
            P("sweep"),
            P("row", "col"),
            P(("sweep", "dp", "row"), "col"),
            P("col", "row"),
            P("col", "row"),
            P("row", "col"),
        ),
        out_specs=(
            P(("sweep", "col"), ("row", "dp")),
            P(("sweep", "col"), ("row", "dp")),
            P(("sweep", "row"), ("col", "dp")),
        ),
        check_vma=False,
    )
```

```python
import functools

import jax
import jax.numpy as jnp
from jax import lax
from jax.experimental import pallas as pl
from jax.experimental.pallas import tpu as pltpu
from jax.sharding import PartitionSpec as P

MESH = pl.DeviceIdType.MESH
BF16 = jnp.bfloat16
F32 = jnp.float32
LANES = 128
PACK = 16


FIRST = (
    (),
    (),
    ("w1",),
    ("w2",),
    ("w0",),
    (),
    (),
    (),
)
SECOND = (
    ("x0",),
    ("x1", "c0",),
    ("x2", "fS0", "c1",),
    ("x3", "c2", "fR0", "bS0", "fF0",),
    ("x4", "c3", "bR0", "fS1", "fP0", "bF0",),
    ("x5", "c4", "fR1", "bS1", "bP0", "c5", "fF1",),
    ("x6", "bR1", "fS2", "c6", "fP1", "bF1",),
    ("x7", "fR2", "bS2", "c7", "bP1", "fF2",),
    ("x8", "bR2", "fS3", "c8", "bS3", "fP2", "bF2", "G0",),
    ("fR3", "bR3", "bP2", "bF3", "fF3", "G1",),
    ("bP3", "fP3", "G2", "A3", "G3",),
)


TURN = (0, 1, 2, 2, 2, 2, 3, 4, 5, 5, 6, 6)


def up_to(n, m):
    return -(-n // m) * m


def dot_nt(a, b):
    return lax.dot_general(a, b, (((1,), (1,)), ((), ())), preferred_element_type=F32)


def dot_nn(a, b):
    return lax.dot_general(a, b, (((1,), (0,)), ((), ())), preferred_element_type=F32)


def arrival_order(nz):
    order = [0]
    for s in range(1, nz // 2):
        order += [-s, s]
    return order + [nz // 2]


def kernel(
    nz, nx, hid,
    ids_ref, index_ref, table_hbm, cot_ref, gate_hbm, up_hbm, down_hbm,
    gg_ref, gu_ref, gd_ref,
    ids, table_ref, gate_w, up_w, down_w, w, look, rs_left, rs_right, xs, cs,
    bp32, bp16, brelay, bcomb, barrived, bsum,
    fp32, fp16, frelay, fcomb, farrived, fsum,
    acts, hid_other,
    t_sem, w_sem, rs_send, rs_recv, c_send, c_recv, x_send, x_recv, dp_send, dp_recv,
    br_send, br_recv, fr_send, fr_recv, hid_send, hid_recv,
):
    z, x, c = lax.axis_index("row"), lax.axis_index("col"), lax.axis_index("dp")
    up_z, down_z = lax.rem(z + 1, nz), lax.rem(z + nz - 1, nz)
    right, left, far = lax.rem(x + 1, nx), lax.rem(x + nx - 1, nx), lax.rem(x + 2, nx)
    other = 1 - c
    half = nz // 2
    order = arrival_order(nz)
    slot_of = {d % nz: p for p, d in enumerate(order)}
    groups = nz // nx
    width = bp32.shape[2]
    rows = cot_ref.shape[0]
    feat = cot_ref.shape[1]
    lanes = 2 * rows
    fetches = [
        pltpu.make_async_copy(src, dst, w_sem.at[n])
        for n, (src, dst) in enumerate(((down_hbm, down_w), (gate_hbm, gate_w), (up_hbm, up_w)))
    ]
    entries = table_hbm.shape[0]
    step = up_to(entries // 8, 8)
    parts = [
        pltpu.make_async_copy(table_hbm.at[a : min(a + step, entries)], table_ref.at[a : min(a + step, entries)], t_sem.at[n])
        for n, a in enumerate(range(0, entries, step))
    ]
    for copy in parts:
        copy.start()

    def send(src, dst, ssem, rsem, **where):
        copy = pltpu.make_async_remote_copy(
            src_ref=src, dst_ref=dst, send_sem=ssem, recv_sem=rsem,
            device_id=where, device_id_type=MESH,
        )
        copy.start()

    def sent(ref, ssem):
        pltpu.make_async_remote_copy(
            src_ref=ref, dst_ref=ref, send_sem=ssem, recv_sem=ssem,
            device_id={"dp": other}, device_id_type=MESH,
        ).wait_send()

    def landed(dst, rsem):
        pltpu.make_async_remote_copy(
            src_ref=dst, dst_ref=dst, send_sem=rsem, recv_sem=rsem,
            device_id={"dp": other}, device_id_type=MESH,
        ).wait_recv()

    barrier = pltpu.get_barrier_semaphore()
    for where in ({"row": up_z}, {"row": down_z}, {"col": left}, {"col": right}, {"dp": other}):
        pl.semaphore_signal(barrier, inc=1, device_id=where, device_id_type=MESH)

    for t in range(ids_ref.shape[0]):
        wide = jnp.broadcast_to(ids_ref[t : t + 1], (LANES, LANES))
        ids[t * LANES : (t + 1) * LANES] = wide.T - z * table_ref.shape[0]
    k_in = jnp.full((1, feat), index_ref[0].astype(F32), F32)
    k_out = jnp.full((1, LANES), index_ref[1].astype(F32), F32)
    in_mult = jnp.exp2(k_in / 2.0 - 1.5)
    out_mult = jnp.exp2(1.0 - k_out / 2.0)

    def lookup(offsets):
        picks = []
        for d in offsets:
            at = pl.ds(pl.multiple_of(lax.rem(z + d + nz, nz) * rows, rows), rows)
            wide = jnp.concatenate([ids[at]] * (up_to(entries, LANES) // LANES), axis=1)[:, :entries]
            spot = lax.broadcasted_iota(jnp.int32, (rows, entries), 1)
            picks.append(jnp.where(spot == wide, 1.0, 0.0).astype(BF16))
        found = dot_nn(jnp.concatenate(picks, axis=0), table_ref[...])
        scaled = (in_mult * found).astype(BF16)
        for n, d in enumerate(offsets):
            look[d % nz] = scaled[n * rows : (n + 1) * rows]

    for copy in parts:
        copy.wait()
    for fetch in fetches:
        fetch.start()
    lookup((-half, half - 1))
    cs[0, c] = cot_ref[...]
    pl.semaphore_wait(barrier, 5)

    c_up, c_down = half, half - 1
    x_up, x_down = half - 1, half
    ways = ((0, up_z), (1, down_z))

    def slot_at(way, s):
        return slot_of[(-s if way == 0 else s) % nz]

    def c_ring(s):
        for way, where in ways:
            n = (c_up, c_down)[way]
            if s > n:
                continue
            slot = slot_at(way, s)
            if s > 0:
                landed(cs.at[slot, c], c_recv.at[way, s - 1])
            if s > 0 or way == 0:
                send(cs.at[slot, c], cs.at[slot, c], dp_send.at[0], dp_recv.at[0, slot // nx], dp=other)
            if s < n:
                send(cs.at[slot, c], cs.at[slot_at(way, s + 1), c], c_send.at[0], c_recv.at[way, s], row=where)

    def x_ring(s):
        for h in range(2):
            cut = pl.ds(h * (rows // 2), rows // 2)
            for way, where in ways:
                n = (x_up, x_down)[way]
                if s > n:
                    continue
                slot = slot_at(way, s)
                if s > 0:
                    landed(xs.at[slot, c, cut], x_recv.at[way, s - 1, h])
                if s > 0 or way == 0:
                    send(xs.at[slot, c, cut], xs.at[slot, c, cut], dp_send.at[1], dp_recv.at[1, slot // nx], dp=other)
                if s < n:
                    send(xs.at[slot, c, cut], xs.at[slot_at(way, s + 1), c, cut],
                         x_send.at[0], x_recv.at[way, s, h], row=where)

    class Sums:
        def __init__(self, kind, first, bufs, sems, tokens):
            self.kind, self.first, self.tokens = kind, first, tokens
            self.p32, self.p16, self.relay, self.comb, self.arrived, self.sum = bufs
            self.ssem, self.rsem = sems
            self.tall = self.p32.shape[2]
            self.top, self.low = pl.ds(0, self.tall // 2), pl.ds(self.tall // 2, self.tall // 2)

        def go(self, g, n, src, dst, **where):
            send(src, dst, self.ssem.at[1 if n in (6, 7, 10, 11) else 0], self.rsem.at[g, TURN[n]], **where)

        def got(self, g, n, dst):
            landed(dst, self.rsem.at[g, TURN[n]])

        def start(self, g):
            landed(self.tokens.at[g * nx : (g + 1) * nx, other], dp_recv.at[self.kind, g])
            pair = 2

            def tokens_of(t, carry):
                tokens = self.tokens[pl.ds(g * nx + t * pair, pair)].reshape(pair * lanes, feat)
                val = dot_nt(w[self.first : self.first + self.tall], tokens)
                for i in range(pair):
                    block = val[:, i * lanes : (i + 1) * lanes]
                    self.p32[g, t * pair + i] = block
                    self.p16[g, t * pair + i] = block.astype(BF16)
                return carry

            lax.fori_loop(0, nx // pair, tokens_of, 0)
            top, low = self.top, self.low
            self.go(g, 0, self.p16.at[g, far, top], self.relay.at[g, 0], col=right)
            self.go(g, 1, self.p16.at[g, far, low], self.relay.at[g, 1], col=left)
            self.go(g, 2, self.p16.at[g, right, low], self.arrived.at[g, 0, low], col=right)
            self.go(g, 3, self.p16.at[g, left, top], self.arrived.at[g, 1, top], col=left)

        def relay_sums(self, g):
            top, low = self.top, self.low
            self.got(g, 0, self.relay.at[g, 0])
            self.comb[g, 0] = (self.p32[g, right, top] + self.relay[g, 0].astype(F32)).astype(BF16)
            self.go(g, 4, self.comb.at[g, 0], self.arrived.at[g, 0, top], col=right)
            self.got(g, 1, self.relay.at[g, 1])
            self.comb[g, 1] = (self.p32[g, left, low] + self.relay[g, 1].astype(F32)).astype(BF16)
            self.go(g, 5, self.comb.at[g, 1], self.arrived.at[g, 1, low], col=left)

        def finish(self, g):
            self.got(g, 2, self.arrived.at[g])
            total = self.p32[g, x] + self.arrived[g, 0].astype(F32) + self.arrived[g, 1].astype(F32)
            if self.kind == 0:
                total = out_mult[:, :lanes] * total
            self.sum[g, x] = total.astype(BF16)
            top, low = self.top, self.low
            self.go(g, 6, self.sum.at[g, x, top], self.sum.at[g, x, top], col=right)
            self.go(g, 7, self.sum.at[g, x, low], self.sum.at[g, x, low], col=left)
            self.go(g, 10, self.sum.at[g, x, low], self.sum.at[g, x, low], col=right)
            self.go(g, 11, self.sum.at[g, x, top], self.sum.at[g, x, top], col=left)

        def pass_on(self, g):
            top, low = self.top, self.low
            self.got(g, 6, self.sum.at[g, left, top])
            self.go(g, 8, self.sum.at[g, left, top], self.sum.at[g, left, top], col=right)
            self.got(g, 7, self.sum.at[g, right, low])
            self.go(g, 9, self.sum.at[g, right, low], self.sum.at[g, right, low], col=left)

        def near(self, g):
            self.got(g, 10, self.sum.at[g, left])

        def gathered(self, g):
            self.got(g, 8, self.sum.at[g, far])

        def drained(self):
            sent(self.p16, self.ssem.at[0])
            sent(self.arrived, self.ssem.at[1])

    back_sums = Sums(0, 2 * width, (bp32, bp16, brelay, bcomb, barrived, bsum), (br_send, br_recv), cs)
    fwd_sums = Sums(1, 0, (fp32, fp16, frelay, fcomb, farrived, fsum), (fr_send, fr_recv), xs)

    def weight_rows(n, src, first):
        fetches[n].wait()
        w[first + width - PACK : first + width] = jnp.zeros((PACK, feat), BF16)
        for core in range(2):

            @pl.when(c == core)
            def _():
                mine = slice(core * hid, (core + 1) * hid)
                w[first : first + hid] = src[mine]

    def activate(g, q):
        gate = fsum[g, q, :width].astype(F32)
        up = fsum[g, q, width:].astype(F32)
        back = bsum[g, q].astype(F32)
        sig = jax.nn.sigmoid(gate)
        silu = gate * sig
        acts[g, q, :width] = (silu * up).astype(BF16)
        acts[g, q, width : 2 * width] = (back * up * sig * (1.0 + gate * (1.0 - sig))).astype(BF16)
        acts[g, q, 2 * width :] = (back * silu).astype(BF16)
        send(acts.at[g, q, 0:width], hid_other.at[g, q], hid_send.at[0], hid_recv.at[g], dp=other)

    def near_activations(g):
        back_sums.near(g)
        back_sums.gathered(g)
        fwd_sums.near(g)

        def one(t, carry):
            activate(g, lax.rem(x + nx - 1 + t, nx))
            return carry

        lax.fori_loop(0, nx - 1, one, 0)

    def gradients(g):
        last = g == groups - 1
        if not last:
            near_activations(g)
        fwd_sums.gathered(g)
        activate(g, far)
        quarter = feat // 4
        slots = slice(g * nx, (g + 1) * nx)

        def product(left_side, tokens, feats):
            return dot_nn(left_side, tokens[slots, :, :, feats].reshape(nx * lanes, quarter))

        def along_tokens(pieces):
            return jnp.concatenate(pieces, axis=1)

        def sides(t, carry):
            feats = pl.ds(pl.multiple_of(t * quarter, LANES), quarter)
            val = product(along_tokens([acts[g, q, width:] for q in range(nx)]), xs, feats)
            for out, first in ((gg_ref, 0), (gu_ref, width)):
                part = val[first : first + hid]
                out[:, feats] = part if g == 0 else out[:, feats] + part
            return carry

        lax.fori_loop(0, 4, sides, 0)
        landed(hid_other.at[g], hid_recv.at[g])

        def down(t, carry):
            feats = pl.ds(pl.multiple_of((2 * c + t) * quarter, LANES), quarter)
            to = pl.ds(pl.multiple_of(t * quarter, LANES), quarter)
            mine = along_tokens([acts[g, q, :width] for q in range(nx)])
            theirs = along_tokens([hid_other[g, q] for q in range(nx)])
            val = product(jnp.concatenate([mine, theirs], axis=0), cs, feats)
            for core, first in ((c, 0), (other, width)):
                at = pl.ds(pl.multiple_of(core * hid, 8), hid)
                part = val[first : first + hid]
                if g > 0:
                    part = part + gd_ref[at, to]
                gd_ref[at, to] = out_mult[:, :1] * part if last else part
            return carry

        lax.fori_loop(0, 2, down, 0)

    pieces = 4
    part = rows // pieces

    def rs_step(s):
        down_d, up_d = s - 1 - half, half - s
        for h in range(pieces):
            cut = pl.ds(h * part, part)
            if s > 1:
                landed(rs_left.at[s - 2, cut], rs_recv.at[0, s - 2, h])
                look[down_d % nz, cut] = look[down_d % nz, cut] + rs_left[s - 2, cut]
            send(look.at[down_d % nz, cut], rs_left.at[s - 1, cut],
                 rs_send.at[0], rs_recv.at[0, s - 1, h], row=down_z)
            if s < half:
                if s > 1:
                    landed(rs_right.at[s - 2, cut], rs_recv.at[1, s - 2, h])
                    look[up_d % nz, cut] = look[up_d % nz, cut] + rs_right[s - 2, cut]
                send(look.at[up_d % nz, cut], rs_right.at[s - 1, cut],
                     rs_send.at[1], rs_recv.at[1, s - 1, h], row=up_z)

    calls = {
        "w": lambda g: weight_rows(*((0, down_w, 2 * width), (1, gate_w, 0), (2, up_w, width))[g]),
        "c": c_ring, "x": x_ring, "A": near_activations, "G": gradients,
        "bS": back_sums.start, "bR": back_sums.relay_sums, "bF": back_sums.finish, "bP": back_sums.pass_on,
        "fS": fwd_sums.start, "fR": fwd_sums.relay_sums, "fF": fwd_sums.finish, "fP": fwd_sums.pass_on,
    }

    def run(line):
        for item in line:
            name, n = item[:-1], int(item[-1])
            calls[name](n)

    for s in range(1, half + 1):
        rs_step(s)
        if s < half:
            lookup((s - half, half - s - 1))
        run(FIRST[s - 1])

    for h in range(pieces):
        cut = pl.ds(h * part, part)
        landed(rs_left.at[half - 1, cut], rs_recv.at[0, half - 1, h])
        landed(rs_right.at[half - 2, cut], rs_recv.at[1, half - 2, h])
        xs[0, c, cut] = look[0, cut] + rs_left[half - 1, cut] + rs_right[half - 2, cut]
    for line in SECOND:
        run(line)

    sent(rs_left, rs_send.at[0])
    sent(rs_right.at[: half - 1], rs_send.at[1])
    for sem in (c_send, x_send):
        sent(look.at[: nz - 1], sem.at[0])
    for k in range(2):
        sent(look, dp_send.at[k])
    back_sums.drained()
    fwd_sums.drained()
    sent(hid_other, hid_send.at[0])


def solution(mesh):
    nz, nx, nc = mesh.shape["row"], mesh.shape["col"], mesh.shape["dp"]

    def local(token_ids, sweep_index, table, cotangent, gate_weight, up_weight, down_weight):
        hid = gate_weight.shape[1] // nc
        feat = table.shape[1]
        rows = cotangent.shape[0]
        width = up_to(hid, 2 * PACK)
        groups, half, slots = nz // nx, nz // 2, nz
        lanes = nc * rows
        dma = pltpu.SemaphoreType.DMA
        vmem = pl.BlockSpec(memory_space=pltpu.VMEM)
        smem = pl.BlockSpec(memory_space=pltpu.SMEM)
        hbm = pl.BlockSpec(memory_space=pl.ANY)

        def sums(tall):
            return [
                pltpu.VMEM((groups, nx, tall, lanes), F32),
                pltpu.VMEM((groups, nx, tall, lanes), BF16),
                pltpu.VMEM((groups, 2, tall // 2, lanes), BF16),
                pltpu.VMEM((groups, 2, tall // 2, lanes), BF16),
                pltpu.VMEM((groups, 2, tall, lanes), BF16),
                pltpu.VMEM((groups, nx, tall, lanes), BF16),
            ]

        shapes = ((hid, feat), (hid, feat), (nc * hid, feat // nc))
        grad_gate, grad_up, grad_down = pl.pallas_call(
            functools.partial(kernel, nz, nx, hid),
            out_shape=tuple(pltpu.VMEM(shape, F32) for shape in shapes),
            in_specs=[vmem, smem, hbm, vmem, hbm, hbm, hbm],
            out_specs=(vmem, vmem, vmem),
            scratch_shapes=[
                pltpu.VMEM((nz * rows, LANES), jnp.int32),
                pltpu.VMEM(table.shape, BF16),
                pltpu.VMEM(down_weight.shape, BF16),
                pltpu.VMEM(down_weight.shape, BF16),
                pltpu.VMEM(down_weight.shape, BF16),
                pltpu.VMEM((3 * width, feat), BF16),
                pltpu.VMEM((nz, rows, feat), BF16),
                pltpu.VMEM((half, rows, feat), BF16),
                pltpu.VMEM((half, rows, feat), BF16),
                pltpu.VMEM((slots, nc, rows, feat), BF16),
                pltpu.VMEM((slots, nc, rows, feat), BF16),
                *sums(width),
                *sums(2 * width),
                pltpu.VMEM((groups, nx, 3 * width, lanes), BF16),
                pltpu.VMEM((groups, nx, width, lanes), BF16),
                dma((8,)), dma((3,)),
                dma((2,)), dma((2, half, 4)),
                dma((1,)), dma((2, half)),
                dma((1,)), dma((2, half, 2)),
                dma((2,)), dma((2, groups)),
                dma((2,)), dma((groups, 7)),
                dma((2,)), dma((groups, 7)),
                dma((1,)), dma((groups,)),
            ],
            compiler_params=pltpu.CompilerParams(
                collective_id=0, has_side_effects=True, vmem_limit_bytes=58 * 1024 * 1024,
            ),
        )(token_ids.reshape(-1, LANES), sweep_index, table, cotangent, gate_weight.T, up_weight.T, down_weight)
        return grad_gate.T, grad_up.T, grad_down

    return jax.shard_map(
        local,
        mesh=mesh,
        in_specs=(
            P(("sweep", "dp")),
            P("sweep"),
            P("row", "col"),
            P(("sweep", "dp", "row"), "col"),
            P("col", "row"),
            P("col", "row"),
            P("row", "col"),
        ),
        out_specs=(
            P(("sweep", "col"), ("row", "dp")),
            P(("sweep", "col"), ("row", "dp")),
            P(("sweep", "row"), ("col", "dp")),
        ),
        check_vma=False,
    )
```
